32 devices in a mesh: section: 2 (over core), egroup: 4 (over y, x), fsdp: 4 (over z).
Axes of the slice: x: 2, y: 2, z: 4, core: 2. Of those that a mesh axis runs over, the one named last changes fastest.
Arguments:
- tokens: bfloat16 [4096, 2048], P(('section', 'egroup', 'fsdp')), may hold values from -6 to 6
- expert_ids: int32 [4096, 2], P(('section', 'egroup', 'fsdp')), may hold values from 0 to 3, all different within a row; in each aligned block of 128 rows (0 to 127, 128 to 255, ...) at most 96 rows name the same one
- gate_weights: float32 [4096, 2], P(('section', 'egroup', 'fsdp')), may hold values from 0.25 to 1
- w_in: bfloat16 [4, 2048, 4096], P('egroup', 'fsdp', 'section'), may hold values from -0.125 to 0.125
- w_out: bfloat16 [4, 4096, 2048], P('egroup', 'section', 'fsdp'), may hold values from -0.09375 to 0.09375
Outputs:
- mixed: bfloat16 [4096, 2048], P(('section', 'egroup', 'fsdp'))
The draws below stay inside these ranges and needn't reach their ends.
Inputs may be any that keep to these rules, and one draw needn't show every extreme that they name: `expert_ids`: the two experts of a token differ. Among the 128 tokens of one device (aligned blocks of rows), at most 96 name any one expert, a bound that some block reaches.
All inputs are finite; a program needn't handle non-finite values.
Results may differ from the reference program's by a relative error of at most 0.0065.
Values may be sent and summed in bfloat16 or wider, within the bound.
A program may use at most 128 MiB of HBM per device.

```python
import math
import jax
import jax.numpy as jnp
import numpy as np
from jax import lax

D = 2048
FF = 4096
TOK_DEV = 128
EXPERTS = 4
CAP = 96
TOKENS = 4096
N_SECTION = 2
DEVICES = 32


def levels(stream_key, dims, split, smallest, high):
    def one(position, blocks):
        draws = jax.random.uniform(jax.random.fold_in(jax.random.fold_in(stream_key, 6), position), (blocks,), jnp.float32, smallest / len(split), high / len(split))
        return jnp.repeat(jnp.exp(draws), dims[position] // blocks).reshape((-1,) + (1,) * (len(dims) - position - 1))

    loudness = one(*split[0])
    for cut in split[1:]:
        loudness = loudness * one(*cut)
    return loudness


def routed_block(stream_key, own, number, rows, count, top, most, lean):
    order = jax.random.permutation(stream_key, count)
    packed, ordinary = portions_of(count, rows * top, most, lean, True), portions_of(count, rows * top, most, lean, False)
    places = jnp.arange(count)

    def named(sizes, rotation):
        used = int((sizes > 0).sum())
        fixed = max(1, used // 4)
        moved = fixed + (places - fixed + rotation * (used - fixed)) % max(1, count - fixed)
        return jnp.zeros((count,), jnp.int32).at[order[jnp.where(places < fixed, places, moved)]].set(jnp.asarray(sizes, jnp.int32))

    sizes = jnp.where(number % 4 == 0, named(packed, number // 4), named(ordinary, number - number // 4 - 1))
    mixed = jax.random.permutation(jax.random.fold_in(own, 3), count)
    source_of, taker = mixed[0:count // 2 * 2:2], mixed[1:count // 2 * 2:2]
    slack = jnp.minimum(sizes[source_of] - 1, most - sizes[taker]) // 2
    slack = jnp.where((source_of == order[0]) | (taker == order[0]) | (sizes[taker] == 0), 0, jnp.maximum(slack, 0))
    moved = jax.random.randint(jax.random.fold_in(own, 4), (count // 2,), 0, 1 << 20) % (slack + 1)
    sizes = sizes.at[source_of].add(-moved).at[taker].add(moved)
    items = jnp.searchsorted(jnp.cumsum(sizes), jnp.arange(rows * top), side="right").astype(jnp.int32)
    grid = items.reshape(top, rows).T
    grid = grid[jax.random.permutation(jax.random.fold_in(own, 1), rows)]
    rotation = jax.random.randint(jax.random.fold_in(own, 2), (rows, 1), 0, top)
    return jnp.take_along_axis(grid, (jnp.arange(top)[None, :] + rotation) % top, axis=1)


def portions_of(count, total, bound, slope, full):
    loads = [(1 << 20) // math.isqrt(rank ** slope) + 1 for rank in range(1, count + 1)]
    largest = bound if full else min(bound, max(-(-total // count), total * loads[0] // sum(loads)))
    least = 1 if total - largest >= count - 1 else 0
    holding, spare = [largest] + [least] * (count - 1), total - largest - least * (count - 1)
    while spare > 0:
        movable = [i for i in range(1, count) if holding[i] < largest] or [i for i in range(1, count) if holding[i] < bound]
        mass, remaining = sum([loads[i] for i in movable]), spare
        for i in movable:
            more = min(bound - holding[i], max(1, remaining * loads[i] // mass), spare)
            holding[i] = holding[i] + more
            spare = spare - more
    return np.array(holding)


def noise(rng, dims, spread, most, split=(), held_as=jnp.bfloat16):
    drawn = jax.random.normal(rng, dims, jnp.float32) * spread
    if len(split) > 0:
        drawn = levels(rng, dims, split, -0.22, 0.18) * drawn
    return jnp.clip(drawn, min=-most, max=most).astype(held_as)


def setup_inputs(seed: int = 0) -> dict:
    seeds = jax.random.split(jax.random.key(seed), 6)
    tokens = noise(seeds[0], (TOKENS, D), 1.0, 6.0, ((0, 32),))
    expert_ids_keys = jax.random.split(jax.random.fold_in(seeds[1], 1), TOKENS // TOK_DEV)
    expert_ids_turns = jax.random.permutation(jax.random.fold_in(seeds[1], 3), TOKENS // TOK_DEV)
    expert_ids = jax.vmap(lambda own, number: routed_block(jax.random.fold_in(seeds[1], 2), own, number, TOK_DEV, EXPERTS, 2, CAP, 1))(expert_ids_keys, expert_ids_turns).reshape((TOKENS, 2))
    gate_weights = jnp.clip(0.25 + 0.75 * jax.random.uniform(seeds[2], (TOKENS, 2), jnp.float32) ** levels(seeds[2], (TOKENS, 2), ((0, 32),), -0.2, 0.2), 0.25, 1.0)
    w_in = noise(seeds[3], (EXPERTS, D, FF), D ** -0.5, 0.125, ((0, 4), (1, 4), (2, 2)))
    w_out = noise(seeds[4], (EXPERTS, FF, D), FF ** -0.5, 0.09375, ((0, 4), (1, 2), (2, 4)))
    return {"tokens": tokens, "expert_ids": expert_ids, "gate_weights": gate_weights, "w_in": w_in, "w_out": w_out}


def reference(tokens, expert_ids, gate_weights, w_in, w_out):
    flat_ids = expert_ids.reshape(-1)
    rows_total = flat_ids.shape[0]
    limit = DEVICES * CAP
    half_width = FF // N_SECTION

    def per_expert(expert, out_rows):
        matched = flat_ids == expert
        row_index = jnp.nonzero(matched, size=limit, fill_value=rows_total)[0].astype(jnp.int32)
        clipped = jnp.minimum(row_index, rows_total - 1)
        is_live = row_index < rows_total
        slot_rows = jnp.where(is_live[:, None], tokens[clipped // 2], jnp.zeros_like(tokens[clipped // 2]))
        first_weight = lax.dynamic_index_in_dim(w_in, expert, 0, keepdims=False)
        second_weight = lax.dynamic_index_in_dim(w_out, expert, 0, keepdims=False)
        hidden = jnp.dot(slot_rows, first_weight, preferred_element_type=jnp.float32)
        activated = jax.nn.gelu(hidden, approximate=False).astype(jnp.bfloat16)
        result = jnp.zeros((limit, D), jnp.float32)
        for section in range(N_SECTION):
            act_part = activated[:, section * half_width:(section + 1) * half_width]
            weight_part = second_weight[section * half_width:(section + 1) * half_width]
            piece = jnp.dot(act_part, weight_part, preferred_element_type=jnp.float32).astype(jnp.bfloat16)
            result = result + piece.astype(jnp.float32)
        return out_rows.at[row_index].set(result.astype(jnp.bfloat16), mode="drop")

    out_rows = jnp.zeros((rows_total, D), jnp.bfloat16)
    out_rows = lax.fori_loop(0, EXPERTS, per_expert, out_rows)
    picked = out_rows.reshape(TOKENS, 2, D).astype(jnp.float32)
    return jnp.sum(gate_weights[:, :, None] * picked, axis=1).astype(jnp.bfloat16)
```

```python
import jax
import jax.numpy as jnp
from jax import lax
from jax.sharding import PartitionSpec as P

EVERY = ("section", "egroup", "fsdp")


def per_device(tokens, expert_ids, gate_weights, w_in, w_out):
    rows, width = tokens.shape
    devices = lax.axis_size("section") * lax.axis_size("egroup") * lax.axis_size("fsdp")
    chunks = 4
    step = rows // chunks
    mine = lax.axis_index("egroup")
    first = lax.all_to_all(w_in[0], "fsdp", split_axis=1, concat_axis=0, tiled=True)
    second = lax.all_to_all(w_out[0], "fsdp", split_axis=0, concat_axis=1, tiled=True)
    ids = lax.all_gather(expert_ids, EVERY, axis=0)
    gates = lax.all_gather(gate_weights, EVERY, axis=0)
    weight = jnp.sum(jnp.where(ids == mine, gates, 0.0), axis=2)
    outs = []
    for chunk in range(chunks):
        part = tokens[chunk * step:(chunk + 1) * step]
        part = lax.all_gather(part, "fsdp", axis=0, tiled=True)
        part = lax.all_gather(part, ("section", "egroup"), axis=0, tiled=True)
        hidden = jnp.dot(part, first, preferred_element_type=jnp.float32)
        activated = jax.nn.gelu(hidden, approximate=False).astype(jnp.bfloat16)
        result = jnp.dot(activated, second, preferred_element_type=jnp.float32)
        scale = weight[:, chunk * step:(chunk + 1) * step].reshape(devices * step, 1)
        result = (result * scale).astype(jnp.bfloat16)
        result = lax.psum_scatter(result, ("section", "egroup"), scatter_dimension=0, tiled=True)
        result = lax.psum_scatter(result, "fsdp", scatter_dimension=0, tiled=True)
        outs.append(result)
    return jnp.concatenate(outs, axis=0)


def solution(mesh):
    placed = (
        P(EVERY, None),
        P(EVERY, None),
        P(EVERY, None),
        P("egroup", "fsdp", "section"),
        P("egroup", "section", "fsdp"),
    )
    return jax.shard_map(
        per_device,
        mesh=mesh,
        in_specs=placed,
        out_specs=P(EVERY, None),
        check_vma=False,
    )
```

```python
import jax
import jax.numpy as jnp
from jax import lax
from jax.experimental import pallas as pl
from jax.experimental.pallas import tpu as pltpu
from jax.sharding import PartitionSpec as P

EVERY = ("section", "egroup", "fsdp")
MESH = pl.DeviceIdType.MESH


def partner(index, step):
    low = index % 2
    high = (index // 2) % 2
    if step % 2:
        index = index + 1 - 2 * low
    if step // 2:
        index = index + 2 - 4 * high
    return index


def gelu(v):
    return 0.5 * v * (1.0 + lax.erf(v * 0.7071067811865476))


def layer_kernel(
    tokens, gates, w_in, w_out, out,
    x, first, second, act, sec, plane, ready, zline, gate_all,
    tz_s, tz_r, tp_s, tp_r, tc_s, tc_r, g_s, g_r, w1_s, w1_r, w2_s, w2_r,
    sec_s, sec_r, pl_s, pl_r, z_s, z_r, loc,
):
    me_s, me_g, me_f = lax.axis_index("section"), lax.axis_index("egroup"), lax.axis_index("fsdp")
    rows, width = tokens.shape
    cols = width // 4
    core = (1 - me_s, me_g, me_f)
    on_plane = [(me_s, partner(me_g, b), me_f) for b in range(4)]
    on_line = [(me_s, me_g, partner(me_f, k)) for k in range(4)]
    partners = [core] + on_plane[1:] + on_line[1:]

    barrier = pltpu.get_barrier_semaphore()
    for device in partners:
        pl.semaphore_signal(barrier, inc=1, device_id=device, device_id_type=MESH)
    pl.semaphore_wait(barrier, len(partners))

    def remote(src, dst, send, recv, device):
        return pltpu.make_async_remote_copy(
            src_ref=src, dst_ref=dst, send_sem=send, recv_sem=recv, device_id=device, device_id_type=MESH
        )

    def block(a, b, k):
        return x.at[a * 4 + b, pl.ds(k * rows, rows), :]

    def piece(weight, p):
        return pl.ds(pl.multiple_of(p * (weight // 4), 128), weight // 4)

    hid = w_in.shape[2]
    token_line = [None] + [
        remote(tokens, block(0, 0, k), tz_s.at[k], tz_r.at[k], on_line[k]) for k in range(1, 4)
    ]
    token_plane = {
        (b, k): remote(
            tokens if k == 0 else block(0, 0, k), block(0, b, k), tp_s.at[b, k], tp_r.at[b, k], on_plane[b]
        )
        for b in range(1, 4)
        for k in range(4)
    }
    token_core = {
        (b, k): remote(
            tokens if b + k == 0 else block(0, b, k), block(1, b, k), tc_s.at[b, k], tc_r.at[b, k], core
        )
        for b in range(4)
        for k in range(4)
    }
    gate_line = [None] + [
        remote(gates, gate_all.at[k], g_s.at[k], g_r.at[k], on_line[k]) for k in range(1, 4)
    ]
    first_line = [None] + [
        remote(
            w_in.at[0, :, piece(hid, partner(me_f, k))], first.at[me_f], w1_s.at[k], w1_r.at[k], on_line[k]
        )
        for k in range(1, 4)
    ]
    second_line = [None] + [
        remote(
            w_out.at[0, piece(hid, partner(me_f, k)), :], second.at[k], w2_s.at[k], w2_r.at[k], on_line[k]
        )
        for k in range(1, 4)
    ]
    own_first = pltpu.make_async_copy(w_in.at[0, :, piece(hid, me_f)], first.at[me_f], loc.at[0])
    own_second = pltpu.make_async_copy(w_out.at[0, piece(hid, me_f), :], second.at[0], loc.at[1])

    for k in (3, 2, 1):
        token_line[k].start()
    for b in range(1, 4):
        token_plane[b, 0].start()
    token_core[0, 0].start()
    for k in (3, 2, 1):
        first_line[k].start()
    for k in (3, 2, 1):
        gate_line[k].start()
    own_first.start()
    own_second.start()
    x[0, 0:rows, :] = tokens[...]
    gate_all[0, :, :] = gates[...]

    for k in (1, 2, 3):
        token_line[k].wait_recv()
        for b in range(1, 4):
            token_plane[b, k].start()
        token_core[0, k].start()
    for k in range(4):
        for b in range(1, 4):
            token_plane[b, k].wait_recv()
            token_core[b, k].start()
    for k in (1, 2, 3):
        first_line[k].wait_recv()
    own_first.wait()
    for k in (1, 2, 3):
        second_line[k].start()

    def project(group, carry):
        hidden = jnp.dot(x[group], first[...].reshape(width, cols), preferred_element_type=jnp.float32)
        act[group] = gelu(hidden).astype(jnp.bfloat16)
        return carry

    lax.fori_loop(0, 4, project, 0)
    for k in range(4):
        for b in range(4):
            token_core[b, k].wait_recv()
    lax.fori_loop(4, 8, project, 0)
    for copy in list(token_plane.values()) + list(token_core.values()):
        copy.wait_send()
    own_second.wait()

    def lane(j):
        return pl.ds(j * cols, cols)

    sec_copy = [remote(x.at[4:8, :, lane(j)], sec.at[j], sec_s.at[j], sec_r.at[j], core) for j in range(4)]
    plane_copy = {
        (j, b): remote(x.at[b, :, lane(j)], plane.at[j, b - 1], pl_s.at[j, b], pl_r.at[j, b], on_plane[b])
        for j in range(4)
        for b in range(1, 4)
    }
    line_copy = {
        (j, k): remote(
            ready.at[j, k], zline.at[j ^ k, k - 1], z_s.at[j, k], z_r.at[j ^ k, k], on_line[k]
        )
        for j in range(4)
        for k in range(1, 4)
    }

    def expand(j):
        if j:
            second_line[j].wait_recv()

        def body(group, carry):
            value = jnp.dot(act[group], second[j], preferred_element_type=jnp.float32)
            x[group, :, j * cols:(j + 1) * cols] = value.astype(jnp.bfloat16)
            return carry

        lax.fori_loop(4, 8, body, 0)
        sec_copy[j].start()
        lax.fori_loop(0, 4, body, 0)

    def join_halves(j):
        sec_copy[j].wait_recv()
        for b in (3, 1, 2, 0):
            total = x[b, :, j * cols:(j + 1) * cols].astype(jnp.float32) + sec[j, b].astype(jnp.float32)
            x[b, :, j * cols:(j + 1) * cols] = total.astype(jnp.bfloat16)
            if b:
                plane_copy[j, b].start()

    def join_experts(j):
        if j == 0:
            for k in (1, 2, 3):
                gate_line[k].wait_recv()
        for b in range(1, 4):
            plane_copy[j, b].wait_recv()
        for k in (3, 2, 1, 0):
            part = slice(k * rows, (k + 1) * rows)
            total = gate_all[k, :, 0:1] * x[0, part, j * cols:(j + 1) * cols].astype(jnp.float32)
            for b in range(1, 4):
                total = total + gate_all[k, :, b:b + 1] * plane[j, b - 1, part, :].astype(jnp.float32)
            ready[j, k] = total.astype(jnp.bfloat16)
            if k:
                line_copy[j, k].start()

    for step in range(6):
        if step < 4:
            expand(step)
        if 0 <= step - 1 < 4:
            join_halves(step - 1)
        if 0 <= step - 2 < 4:
            join_experts(step - 2)
    for j in range(4):
        total = ready[j, 0].astype(jnp.float32)
        for k in range(1, 4):
            line_copy[j ^ k, k].wait_recv()
            total = total + zline[j, k - 1].astype(jnp.float32)
        out[:, pl.ds(pl.multiple_of(partner(me_f, j) * cols, 128), cols)] = total.astype(jnp.bfloat16)

    for copy in token_line[1:] + gate_line[1:] + first_line[1:] + second_line[1:] + sec_copy:
        copy.wait_send()
    for copy in list(plane_copy.values()) + list(line_copy.values()):
        copy.wait_send()


def fused(tokens, expert_ids, gate_weights, w_in, w_out):
    rows, width = tokens.shape
    lanes = jnp.arange(128, dtype=jnp.int32)
    expert = jnp.where(lanes < 4, lanes ^ lax.axis_index("egroup"), -1)[None, :]
    gates = sum(
        jnp.where(expert_ids[:, i:i + 1] == expert, gate_weights[:, i:i + 1], 0.0) for i in range(2)
    )
    cols, hid = width // 4, w_in.shape[2] // 4
    wide, vmem, dma = jnp.bfloat16, pltpu.VMEM, pltpu.SemaphoreType.DMA
    return pl.pallas_call(
        layer_kernel,
        out_shape=jax.ShapeDtypeStruct((rows, width), wide),
        in_specs=[
            pl.BlockSpec(memory_space=pltpu.VMEM),
            pl.BlockSpec(memory_space=pltpu.VMEM),
            pl.BlockSpec(memory_space=pl.ANY),
            pl.BlockSpec(memory_space=pl.ANY),
        ],
        out_specs=pl.BlockSpec(memory_space=pltpu.VMEM),
        scratch_shapes=[
            vmem((8, 4 * rows, width), wide),
            vmem((4, cols, hid), wide),
            vmem((4, hid, cols), wide),
            vmem((8, 4 * rows, hid), wide),
            vmem((4, 4, 4 * rows, cols), wide),
            vmem((4, 3, 4 * rows, cols), wide),
            vmem((4, 4, rows, cols), wide),
            vmem((4, 3, rows, cols), wide),
            vmem((4, rows, 128), jnp.float32),
        ]
        + [dma((4,)), dma((4,)), dma((4, 4)), dma((4, 4)), dma((4, 4)), dma((4, 4)), dma((4,)), dma((4,))]
        + [dma((4,)), dma((4,)), dma((4,)), dma((4,)), dma((4,)), dma((4,))]
        + [dma((4, 4)), dma((4, 4)), dma((4, 4)), dma((4, 4)), dma((2,))],
        compiler_params=pltpu.CompilerParams(
            collective_id=0, has_side_effects=True, vmem_limit_bytes=58 * 2**20
        ),
    )(tokens, gates, w_in, w_out)


def collective(tokens, expert_ids, gate_weights, w_in, w_out):
    rows, width = tokens.shape
    devices = lax.axis_size("section") * lax.axis_size("egroup") * lax.axis_size("fsdp")
    chunks = 4
    step = rows // chunks
    mine = lax.axis_index("egroup")
    first = lax.all_to_all(w_in[0], "fsdp", split_axis=1, concat_axis=0, tiled=True)
    second = lax.all_to_all(w_out[0], "fsdp", split_axis=0, concat_axis=1, tiled=True)
    ids = lax.all_gather(expert_ids, EVERY, axis=0)
    gates = lax.all_gather(gate_weights, EVERY, axis=0)
    weight = jnp.sum(jnp.where(ids == mine, gates, 0.0), axis=2)
    outs = []
    for chunk in range(chunks):
        part = tokens[chunk * step:(chunk + 1) * step]
        part = lax.all_gather(part, "fsdp", axis=0, tiled=True)
        part = lax.all_gather(part, ("section", "egroup"), axis=0, tiled=True)
        hidden = jnp.dot(part, first, preferred_element_type=jnp.float32)
        activated = jax.nn.gelu(hidden, approximate=False).astype(jnp.bfloat16)
        result = jnp.dot(activated, second, preferred_element_type=jnp.float32)
        scale = weight[:, chunk * step:(chunk + 1) * step].reshape(devices * step, 1)
        result = (result * scale).astype(jnp.bfloat16)
        result = lax.psum_scatter(result, ("section", "egroup"), scatter_dimension=0, tiled=True)
        result = lax.psum_scatter(result, "fsdp", scatter_dimension=0, tiled=True)
        outs.append(result)
    return jnp.concatenate(outs, axis=0)


def solution(mesh):
    small = (mesh.shape["section"], mesh.shape["egroup"], mesh.shape["fsdp"]) == (2, 4, 4)
    placed = (
        P(EVERY, None),
        P(EVERY, None),
        P(EVERY, None),
        P("egroup", "fsdp", "section"),
        P("egroup", "section", "fsdp"),
    )
    return jax.shard_map(
        fused if small else collective,
        mesh=mesh,
        in_specs=placed,
        out_specs=P(EVERY, None),
        check_vma=False,
    )
```

```python
import jax
import jax.numpy as jnp
from jax import lax
from jax.experimental import pallas as pl
from jax.experimental.pallas import tpu as pltpu
from jax.sharding import PartitionSpec as P

EVERY = ("section", "egroup", "fsdp")
MESH = pl.DeviceIdType.MESH


def partner(index, step):
    low = index % 2
    high = (index // 2) % 2
    if step % 2:
        index = index + 1 - 2 * low
    if step // 2:
        index = index + 2 - 4 * high
    return index


def gelu(v):
    return 0.5 * v * (1.0 + lax.erf(v * 0.7071067811865476))


def layer_kernel(
    tokens, gates, w_in, w_out, out,
    x, first, second, act, sec, plane, ready, zline, gate_all,
    tz_s, tz_r, tp_s, tp_r, td_s, td_r, tc_s, tc_r, g_s, g_r, w1_s, w1_r, w2_s, w2_r,
    sec_s, sec_r, pl_s, pl_r, z_s, z_r, loc,
):
    me_s, me_g, me_f = lax.axis_index("section"), lax.axis_index("egroup"), lax.axis_index("fsdp")
    rows, width = tokens.shape
    cols = width // 4
    core = (1 - me_s, me_g, me_f)
    on_plane = [(me_s, partner(me_g, b), me_f) for b in range(4)]
    on_line = [(me_s, me_g, partner(me_f, k)) for k in range(4)]
    partners = [core] + on_plane[1:] + on_line[1:]

    barrier = pltpu.get_barrier_semaphore()
    for device in partners:
        pl.semaphore_signal(barrier, inc=1, device_id=device, device_id_type=MESH)
    pl.semaphore_wait(barrier, len(partners))

    def remote(src, dst, send, recv, device):
        return pltpu.make_async_remote_copy(
            src_ref=src, dst_ref=dst, send_sem=send, recv_sem=recv, device_id=device, device_id_type=MESH
        )

    def block(a, b, k):
        return x.at[a * 4 + b, pl.ds(k * rows, rows), :]

    def piece(weight, p):
        return pl.ds(pl.multiple_of(p * (weight // 4), 128), weight // 4)

    hid = w_in.shape[2]
    inner = ((me_f + 1) // 2) % 2
    is_inner = inner == 1
    token_next = remote(tokens, block(0, 0, 1), tz_s.at[1], tz_r.at[1], on_line[1])
    own_across = remote(tokens, block(0, 0, 3), tz_s.at[3], tz_r.at[3], on_line[3])
    end_across = remote(block(0, 0, 1), block(0, 0, 2), tz_s.at[2], tz_r.at[2], on_line[3])
    near_out = remote(block(0, 0, 3), block(0, 0, 2), tz_s.at[4], tz_r.at[2], on_line[1])
    far_out = remote(block(0, 0, 2), block(0, 0, 3), tz_s.at[5], tz_r.at[3], on_line[1])

    def landed(k):
        return remote(tokens, block(0, 0, k), tz_s.at[0], tz_r.at[k], on_line[1])

    def token_plane(b, k, own=False):
        return remote(
            tokens if own else block(0, 0, k), block(0, b, k), tp_s.at[b, k], tp_r.at[b, k], on_plane[b]
        )

    def half(b, k, part):
        return x.at[b, pl.ds(k * rows + part * (rows // 2), rows // 2), :]

    def token_corner(part, k):
        return remote(
            half(1 + part, k, part), half(3, k, part), td_s.at[part, k], td_r.at[part, k], on_plane[2 - part]
        )

    def token_core(b, k, own=False):
        return remote(
            tokens if own else block(0, b, k), block(1, b, k), tc_s.at[b, k], tc_r.at[b, k], core
        )

    gate_line = [None] + [
        remote(gates, gate_all.at[k], g_s.at[k], g_r.at[k], on_line[k]) for k in range(1, 4)
    ]
    first_line = [None] + [
        remote(
            w_in.at[0, :, piece(hid, partner(me_f, k))], first.at[me_f], w1_s.at[k], w1_r.at[k], on_line[k]
        )
        for k in range(1, 4)
    ]
    second_line = [None] + [
        remote(
            w_out.at[0, piece(hid, partner(me_f, k)), :], second.at[k], w2_s.at[k], w2_r.at[k], on_line[k]
        )
        for k in range(1, 4)
    ]
    own_first = pltpu.make_async_copy(w_in.at[0, :, piece(hid, me_f)], first.at[me_f], loc.at[0])
    own_second = pltpu.make_async_copy(w_out.at[0, piece(hid, me_f), :], second.at[0], loc.at[1])

    token_next.start()

    @pl.when(is_inner)
    def _():
        own_across.start()

    for b in (1, 2):
        token_plane(b, 0, True).start()
    token_core(0, 0, True).start()
    for k in (3, 2, 1):
        first_line[k].start()
    for k in (3, 2, 1):
        gate_line[k].start()
    own_first.start()
    own_second.start()
    x[0, 0:rows, :] = tokens[...]
    gate_all[0, :, :] = gates[...]

    def spread(k, onward):
        landed(k).wait_recv()

        @pl.when(is_inner)
        def _():
            onward.start()

        for b in (1, 2):
            token_plane(b, k).start()
        token_core(0, k).start()

    def corner(k):
        for part in range(2):
            token_plane(1 + part, k).wait_recv()
            token_corner(part, k).start()
            token_core(1 + part, k).start()

    second_in = 2 + inner
    third_in = 5 - second_in
    spread(1, end_across)
    corner(0)
    spread(second_in, near_out)
    corner(1)
    spread(third_in, far_out)
    corner(second_in)
    corner(third_in)
    for k in (0, 1, second_in, third_in):
        for part in range(2):
            token_corner(part, k).wait_recv()
        token_core(3, k).start()
    for k in (1, 2, 3):
        first_line[k].wait_recv()
    own_first.wait()
    for k in (1, 2, 3):
        second_line[k].start()

    def project(group, carry):
        hidden = jnp.dot(x[group], first[...].reshape(width, cols), preferred_element_type=jnp.float32)
        act[group] = gelu(hidden).astype(jnp.bfloat16)
        return carry

    lax.fori_loop(0, 4, project, 0)
    for k in range(4):
        for b in range(4):
            token_core(b, k).wait_recv()
    lax.fori_loop(4, 8, project, 0)
    for k in range(4):
        for b in range(4):
            token_core(b, k).wait_send()
        for part in range(2):
            token_plane(1 + part, k).wait_send()
            token_corner(part, k).wait_send()
    token_next.wait_send()

    @pl.when(is_inner)
    def _():
        for copy in (own_across, end_across, near_out, far_out):
            copy.wait_send()

    own_second.wait()

    def lane(j):
        return pl.ds(j * cols, cols)

    sec_copy = [remote(x.at[4:8, :, lane(j)], sec.at[j], sec_s.at[j], sec_r.at[j], core) for j in range(4)]
    plane_copy = {
        (j, b): remote(x.at[b, :, lane(j)], plane.at[j, b - 1], pl_s.at[j, b], pl_r.at[j, b], on_plane[b])
        for j in range(4)
        for b in range(1, 4)
    }
    line_copy = {
        (j, k): remote(
            ready.at[j, k], zline.at[j ^ k, k - 1], z_s.at[j, k], z_r.at[j ^ k, k], on_line[k]
        )
        for j in range(4)
        for k in range(1, 4)
    }

    def expand(j):
        if j:
            second_line[j].wait_recv()

        def body(group, carry):
            value = jnp.dot(act[group], second[j], preferred_element_type=jnp.float32)
            x[group, :, j * cols:(j + 1) * cols] = value.astype(jnp.bfloat16)
            return carry

        lax.fori_loop(4, 8, body, 0)
        sec_copy[j].start()
        lax.fori_loop(0, 4, body, 0)

    def join_halves(j):
        sec_copy[j].wait_recv()
        for b in (3, 1, 2, 0):
            total = x[b, :, j * cols:(j + 1) * cols].astype(jnp.float32) + sec[j, b].astype(jnp.float32)
            x[b, :, j * cols:(j + 1) * cols] = total.astype(jnp.bfloat16)
            if b:
                plane_copy[j, b].start()

    def join_experts(j):
        if j == 0:
            for k in (1, 2, 3):
                gate_line[k].wait_recv()
        for b in range(1, 4):
            plane_copy[j, b].wait_recv()
        for k in (3, 2, 1, 0):
            part = slice(k * rows, (k + 1) * rows)
            total = gate_all[k, :, 0:1] * x[0, part, j * cols:(j + 1) * cols].astype(jnp.float32)
            for b in range(1, 4):
                total = total + gate_all[k, :, b:b + 1] * plane[j, b - 1, part, :].astype(jnp.float32)
            ready[j, k] = total.astype(jnp.bfloat16)
            if k:
                line_copy[j, k].start()

    for step in range(6):
        if step < 4:
            expand(step)
        if 0 <= step - 1 < 4:
            join_halves(step - 1)
        if 0 <= step - 2 < 4:
            join_experts(step - 2)
    for j in range(4):
        total = ready[j, 0].astype(jnp.float32)
        for k in range(1, 4):
            line_copy[j ^ k, k].wait_recv()
            total = total + zline[j, k - 1].astype(jnp.float32)
        out[:, pl.ds(pl.multiple_of(partner(me_f, j) * cols, 128), cols)] = total.astype(jnp.bfloat16)

    for copy in gate_line[1:] + first_line[1:] + second_line[1:] + sec_copy:
        copy.wait_send()
    for copy in list(plane_copy.values()) + list(line_copy.values()):
        copy.wait_send()


def fused(tokens, expert_ids, gate_weights, w_in, w_out):
    rows, width = tokens.shape
    lanes = jnp.arange(128, dtype=jnp.int32)
    expert = jnp.where(lanes < 4, lanes ^ lax.axis_index("egroup"), -1)[None, :]
    gates = sum(
        jnp.where(expert_ids[:, i:i + 1] == expert, gate_weights[:, i:i + 1], 0.0) for i in range(2)
    )
    cols, hid = width // 4, w_in.shape[2] // 4
    wide, vmem, dma = jnp.bfloat16, pltpu.VMEM, pltpu.SemaphoreType.DMA
    return pl.pallas_call(
        layer_kernel,
        out_shape=jax.ShapeDtypeStruct((rows, width), wide),
        in_specs=[
            pl.BlockSpec(memory_space=pltpu.VMEM),
            pl.BlockSpec(memory_space=pltpu.VMEM),
            pl.BlockSpec(memory_space=pl.ANY),
            pl.BlockSpec(memory_space=pl.ANY),
        ],
        out_specs=pl.BlockSpec(memory_space=pltpu.VMEM),
        scratch_shapes=[
            vmem((8, 4 * rows, width), wide),
            vmem((4, cols, hid), wide),
            vmem((4, hid, cols), wide),
            vmem((8, 4 * rows, hid), wide),
            vmem((4, 4, 4 * rows, cols), wide),
            vmem((4, 3, 4 * rows, cols), wide),
            vmem((4, 4, rows, cols), wide),
            vmem((4, 3, rows, cols), wide),
            vmem((4, rows, 128), jnp.float32),
        ]
        + [dma((6,)), dma((4,)), dma((4, 4)), dma((4, 4)), dma((2, 4)), dma((2, 4)), dma((4, 4)), dma((4, 4))]
        + [dma((4,)), dma((4,))]
        + [dma((4,)), dma((4,)), dma((4,)), dma((4,)), dma((4,)), dma((4,))]
        + [dma((4, 4)), dma((4, 4)), dma((4, 4)), dma((4, 4)), dma((2,))],
        compiler_params=pltpu.CompilerParams(
            collective_id=0, has_side_effects=True, vmem_limit_bytes=58 * 2**20
        ),
    )(tokens, gates, w_in, w_out)


def collective(tokens, expert_ids, gate_weights, w_in, w_out):
    rows, width = tokens.shape
    devices = lax.axis_size("section") * lax.axis_size("egroup") * lax.axis_size("fsdp")
    chunks = 4
    step = rows // chunks
    mine = lax.axis_index("egroup")
    first = lax.all_to_all(w_in[0], "fsdp", split_axis=1, concat_axis=0, tiled=True)
    second = lax.all_to_all(w_out[0], "fsdp", split_axis=0, concat_axis=1, tiled=True)
    ids = lax.all_gather(expert_ids, EVERY, axis=0)
    gates = lax.all_gather(gate_weights, EVERY, axis=0)
    weight = jnp.sum(jnp.where(ids == mine, gates, 0.0), axis=2)
    outs = []
    for chunk in range(chunks):
        part = tokens[chunk * step:(chunk + 1) * step]
        part = lax.all_gather(part, "fsdp", axis=0, tiled=True)
        part = lax.all_gather(part, ("section", "egroup"), axis=0, tiled=True)
        hidden = jnp.dot(part, first, preferred_element_type=jnp.float32)
        activated = jax.nn.gelu(hidden, approximate=False).astype(jnp.bfloat16)
        result = jnp.dot(activated, second, preferred_element_type=jnp.float32)
        scale = weight[:, chunk * step:(chunk + 1) * step].reshape(devices * step, 1)
        result = (result * scale).astype(jnp.bfloat16)
        result = lax.psum_scatter(result, ("section", "egroup"), scatter_dimension=0, tiled=True)
        result = lax.psum_scatter(result, "fsdp", scatter_dimension=0, tiled=True)
        outs.append(result)
    return jnp.concatenate(outs, axis=0)


def solution(mesh):
    small = (mesh.shape["section"], mesh.shape["egroup"], mesh.shape["fsdp"]) == (2, 4, 4)
    placed = (
        P(EVERY, None),
        P(EVERY, None),
        P(EVERY, None),
        P("egroup", "fsdp", "section"),
        P("egroup", "section", "fsdp"),
    )
    return jax.shard_map(
        fused if small else collective,
        mesh=mesh,
        in_specs=placed,
        out_specs=P(EVERY, None),
        check_vma=False,
    )
```

```python
import jax
import jax.numpy as jnp
from jax import lax
from jax.experimental import pallas as pl
from jax.experimental.pallas import tpu as pltpu
from jax.sharding import PartitionSpec as P

EVERY = ("section", "egroup", "fsdp")
MESH = pl.DeviceIdType.MESH


def partner(index, step):
    low = index % 2
    high = (index // 2) % 2
    if step % 2:
        index = index + 1 - 2 * low
    if step // 2:
        index = index + 2 - 4 * high
    return index


def gelu(v):
    return 0.5 * v * (1.0 + lax.erf(v * 0.7071067811865476))


def layer_kernel(
    tokens, gates, w_in, w_out, out,
    x, first, second, act, sec, plane, ready, zline, gate_all, scale,
    tz_s, tz_r, tp_s, tp_r, td_s, td_r, tc_s, tc_r, g_s, g_r, w1_s, w1_r, w2_s, w2_r,
    sec_s, sec_r, pl_s, pl_r, z_s, z_r, loc,
):
    me_s, me_g, me_f = lax.axis_index("section"), lax.axis_index("egroup"), lax.axis_index("fsdp")
    rows, width = tokens.shape
    cols = width // 4
    core = (1 - me_s, me_g, me_f)
    on_plane = [(me_s, partner(me_g, b), me_f) for b in range(4)]
    on_line = [(me_s, me_g, partner(me_f, k)) for k in range(4)]
    partners = [core] + on_plane[1:] + on_line[1:]

    barrier = pltpu.get_barrier_semaphore()
    for device in partners:
        pl.semaphore_signal(barrier, inc=1, device_id=device, device_id_type=MESH)
    pl.semaphore_wait(barrier, len(partners))

    def remote(src, dst, send, recv, device):
        return pltpu.make_async_remote_copy(
            src_ref=src, dst_ref=dst, send_sem=send, recv_sem=recv, device_id=device, device_id_type=MESH
        )

    def block(a, b, k):
        return x.at[a * 4 + b, pl.ds(k * rows, rows), :]

    def piece(weight, p):
        return pl.ds(pl.multiple_of(p * (weight // 4), 128), weight // 4)

    hid = w_in.shape[2]
    inner = ((me_f + 1) // 2) % 2
    is_inner = inner == 1
    token_next = remote(tokens, block(0, 0, 1), tz_s.at[1], tz_r.at[1], on_line[1])
    own_across = remote(tokens, block(0, 0, 3), tz_s.at[3], tz_r.at[3], on_line[3])
    end_across = remote(block(0, 0, 1), block(0, 0, 2), tz_s.at[2], tz_r.at[2], on_line[3])
    near_out = remote(block(0, 0, 3), block(0, 0, 2), tz_s.at[4], tz_r.at[2], on_line[1])
    far_out = remote(block(0, 0, 2), block(0, 0, 3), tz_s.at[5], tz_r.at[3], on_line[1])

    def landed(k):
        return remote(tokens, block(0, 0, k), tz_s.at[0], tz_r.at[k], on_line[1])

    def token_plane(b, k, own=False):
        return remote(
            tokens if own else block(0, 0, k), block(0, b, k), tp_s.at[b, k], tp_r.at[b, k], on_plane[b]
        )

    def half(b, k, part):
        return x.at[b, pl.ds(k * rows + part * (rows // 2), rows // 2), :]

    def token_corner(part, k):
        return remote(
            half(1 + part, k, part), half(3, k, part), td_s.at[part, k], td_r.at[part, k], on_plane[2 - part]
        )

    def token_core(b, k, own=False):
        return remote(
            tokens if own else block(0, b, k), block(1, b, k), tc_s.at[b, k], tc_r.at[b, k], core
        )

    gate_line = [None] + [
        remote(gates, gate_all.at[0, k], g_s.at[0, k], g_r.at[0, k], on_line[k]) for k in range(1, 4)
    ]
    gate_plane = {
        (b, k): remote(
            gates if k == 0 else gate_all.at[0, k],
            gate_all.at[b, k],
            g_s.at[b, k],
            g_r.at[b, k],
            on_plane[b],
        )
        for b in range(1, 4)
        for k in range(4)
    }
    first_line = [None] + [
        remote(
            w_in.at[0, :, piece(hid, partner(me_f, k))], first.at[me_f], w1_s.at[k], w1_r.at[k], on_line[k]
        )
        for k in range(1, 4)
    ]
    second_line = [None] + [
        remote(
            w_out.at[0, piece(hid, partner(me_f, k)), :], second.at[k], w2_s.at[k], w2_r.at[k], on_line[k]
        )
        for k in range(1, 4)
    ]
    own_first = pltpu.make_async_copy(w_in.at[0, :, piece(hid, me_f)], first.at[me_f], loc.at[0])
    own_second = pltpu.make_async_copy(w_out.at[0, piece(hid, me_f), :], second.at[0], loc.at[1])

    token_next.start()

    @pl.when(is_inner)
    def _():
        own_across.start()

    for b in (1, 2):
        token_plane(b, 0, True).start()
    token_core(0, 0, True).start()
    for k in (3, 2, 1):
        first_line[k].start()
    for k in (3, 2, 1):
        gate_line[k].start()
    own_first.start()
    own_second.start()
    x[0, 0:rows, :] = tokens[...]
    for b in range(1, 4):
        gate_plane[b, 0].start()
    gate_all[0, 0] = gates[...]

    def spread(k, onward):
        landed(k).wait_recv()

        @pl.when(is_inner)
        def _():
            onward.start()

        for b in (1, 2):
            token_plane(b, k).start()
        token_core(0, k).start()

    def corner(k):
        for part in range(2):
            token_plane(1 + part, k).wait_recv()
            token_corner(part, k).start()
            token_core(1 + part, k).start()

    second_in = 2 + inner
    third_in = 5 - second_in
    spread(1, end_across)
    corner(0)
    spread(second_in, near_out)
    corner(1)
    spread(third_in, far_out)
    corner(second_in)
    corner(third_in)
    for k in (0, 1, second_in, third_in):
        for part in range(2):
            token_corner(part, k).wait_recv()
        token_core(3, k).start()
    for k in (1, 2, 3):
        first_line[k].wait_recv()
    own_first.wait()
    for k in (1, 2, 3):
        second_line[k].start()
    for k in (1, 2, 3):
        gate_line[k].wait_recv()
        for b in range(1, 4):
            gate_plane[b, k].start()

    def project(group, carry):
        hidden = jnp.dot(x[group], first[...].reshape(width, cols), preferred_element_type=jnp.float32)
        act[group] = gelu(hidden).astype(jnp.bfloat16)
        return carry

    lax.fori_loop(0, 4, project, 0)
    for k in range(4):
        for b in range(4):
            token_core(b, k).wait_recv()
    lax.fori_loop(4, 8, project, 0)
    for k in range(4):
        for b in range(4):
            token_core(b, k).wait_send()
        for part in range(2):
            token_plane(1 + part, k).wait_send()
            token_corner(part, k).wait_send()
    token_next.wait_send()

    @pl.when(is_inner)
    def _():
        for copy in (own_across, end_across, near_out, far_out):
            copy.wait_send()

    own_second.wait()

    def lane(j):
        return pl.ds(j * cols, cols)

    sec_copy = [remote(x.at[4:8, :, lane(j)], sec.at[j], sec_s.at[j], sec_r.at[j], core) for j in range(4)]
    def part_rows(part):
        return pl.ds(part * 2 * rows, 2 * rows)

    plane_copy = {}
    for j in range(4):
        for part in range(2):
            near, far = 1 + part, 2 - part
            for i, (group, device) in enumerate(((near, near), (3, near), (far, far))):
                plane_copy[j, part, i] = remote(
                    x.at[group, part_rows(part), lane(j)],
                    plane.at[j, i, part_rows(part), :],
                    pl_s.at[j, part * 3 + i],
                    pl_r.at[j, part * 3 + i],
                    on_plane[device],
                )
    line_copy = {
        (j, k): remote(
            ready.at[j, k], zline.at[j ^ k, k - 1], z_s.at[j, k], z_r.at[j ^ k, k], on_line[k]
        )
        for j in range(4)
        for k in range(1, 4)
    }

    def expand(j):
        if j:
            second_line[j].wait_recv()

        def body(group, carry):
            value = jnp.dot(act[group], second[j], preferred_element_type=jnp.float32)
            x[group, :, j * cols:(j + 1) * cols] = value.astype(jnp.bfloat16)
            return carry

        lax.fori_loop(4, 8, body, 0)
        sec_copy[j].start()
        lax.fori_loop(0, 4, body, 0)

    def join_halves(j):
        if j == 0:
            for b in range(4):
                for k in range(4):
                    if b:
                        gate_plane[b, k].wait_recv()
                    scale[b, k * rows:(k + 1) * rows, :] = jnp.transpose(gate_all[b, k])
        sec_copy[j].wait_recv()
        for b in (3, 1, 2, 0):
            total = x[b, :, j * cols:(j + 1) * cols].astype(jnp.float32) + sec[j, b].astype(jnp.float32)
            total = total * scale[b, :, b:b + 1]
            x[b, :, j * cols:(j + 1) * cols] = total.astype(jnp.bfloat16)
            if b == 3:
                plane_copy[j, 0, 1].start()
                plane_copy[j, 1, 1].start()
            elif b:
                plane_copy[j, b - 1, 0].start()

    def pass_on(j):
        for part in range(2):
            group, span = 2 - part, slice(part * 2 * rows, (part + 1) * 2 * rows)
            plane_copy[j, part, 1].wait_recv()
            total = x[group, span, j * cols:(j + 1) * cols].astype(jnp.float32)
            total = total + plane[j, 1, span, :].astype(jnp.float32)
            x[group, span, j * cols:(j + 1) * cols] = total.astype(jnp.bfloat16)
            plane_copy[j, part, 2].start()

    def join_experts(j):
        for part in range(2):
            plane_copy[j, part, 0].wait_recv()
            plane_copy[j, part, 2].wait_recv()
        for k in (3, 2, 1, 0):
            span = slice(k * rows, (k + 1) * rows)
            total = x[0, span, j * cols:(j + 1) * cols].astype(jnp.float32)
            for i in (0, 2):
                total = total + plane[j, i, span, :].astype(jnp.float32)
            ready[j, k] = total.astype(jnp.bfloat16)
            if k:
                line_copy[j, k].start()

    for step in range(7):
        if 0 <= step - 1 < 4:
            join_halves(step - 1)
        if 0 <= step - 2 < 4:
            pass_on(step - 2)
        if 0 <= step - 3 < 4:
            join_experts(step - 3)
        if step < 4:
            expand(step)
    for j in range(4):
        total = ready[j, 0].astype(jnp.float32)
        for k in range(1, 4):
            line_copy[j ^ k, k].wait_recv()
            total = total + zline[j, k - 1].astype(jnp.float32)
        out[:, pl.ds(pl.multiple_of(partner(me_f, j) * cols, 128), cols)] = total.astype(jnp.bfloat16)

    for copy in gate_line[1:] + first_line[1:] + second_line[1:] + sec_copy:
        copy.wait_send()
    for copy in list(gate_plane.values()) + list(plane_copy.values()) + list(line_copy.values()):
        copy.wait_send()


def fused(tokens, expert_ids, gate_weights, w_in, w_out):
    rows, width = tokens.shape
    steps = jnp.arange(8, dtype=jnp.int32)
    expert = jnp.where(steps < 4, steps ^ lax.axis_index("egroup"), -1)[:, None]
    gates = sum(jnp.where(expert_ids[:, i][None, :] == expert, gate_weights[:, i][None, :], 0.0) for i in range(2))
    cols, hid = width // 4, w_in.shape[2] // 4
    wide, vmem, dma = jnp.bfloat16, pltpu.VMEM, pltpu.SemaphoreType.DMA
    return pl.pallas_call(
        layer_kernel,
        out_shape=jax.ShapeDtypeStruct((rows, width), wide),
        in_specs=[
            pl.BlockSpec(memory_space=pltpu.VMEM),
            pl.BlockSpec(memory_space=pltpu.VMEM),
            pl.BlockSpec(memory_space=pl.ANY),
            pl.BlockSpec(memory_space=pl.ANY),
        ],
        out_specs=pl.BlockSpec(memory_space=pltpu.VMEM),
        scratch_shapes=[
            vmem((8, 4 * rows, width), wide),
            vmem((4, cols, hid), wide),
            vmem((4, hid, cols), wide),
            vmem((8, 4 * rows, hid), wide),
            vmem((4, 4, 4 * rows, cols), wide),
            vmem((4, 3, 4 * rows, cols), wide),
            vmem((4, 4, rows, cols), wide),
            vmem((4, 3, rows, cols), wide),
            vmem((4, 4, 8, rows), jnp.float32),
            vmem((4, 4 * rows, 8), jnp.float32),
        ]
        + [dma((6,)), dma((4,)), dma((4, 4)), dma((4, 4)), dma((2, 4)), dma((2, 4)), dma((4, 4)), dma((4, 4))]
        + [dma((4, 4)), dma((4, 4))]
        + [dma((4,)), dma((4,)), dma((4,)), dma((4,)), dma((4,)), dma((4,))]
        + [dma((4, 6)), dma((4, 6)), dma((4, 4)), dma((4, 4)), dma((2,))],
        compiler_params=pltpu.CompilerParams(
            collective_id=0, has_side_effects=True, vmem_limit_bytes=58 * 2**20
        ),
    )(tokens, gates, w_in, w_out)


def collective(tokens, expert_ids, gate_weights, w_in, w_out):
    rows, width = tokens.shape
    devices = lax.axis_size("section") * lax.axis_size("egroup") * lax.axis_size("fsdp")
    chunks = 4
    step = rows // chunks
    mine = lax.axis_index("egroup")
    first = lax.all_to_all(w_in[0], "fsdp", split_axis=1, concat_axis=0, tiled=True)
    second = lax.all_to_all(w_out[0], "fsdp", split_axis=0, concat_axis=1, tiled=True)
    ids = lax.all_gather(expert_ids, EVERY, axis=0)
    gates = lax.all_gather(gate_weights, EVERY, axis=0)
    weight = jnp.sum(jnp.where(ids == mine, gates, 0.0), axis=2)
    outs = []
    for chunk in range(chunks):
        part = tokens[chunk * step:(chunk + 1) * step]
        part = lax.all_gather(part, "fsdp", axis=0, tiled=True)
        part = lax.all_gather(part, ("section", "egroup"), axis=0, tiled=True)
        hidden = jnp.dot(part, first, preferred_element_type=jnp.float32)
        activated = jax.nn.gelu(hidden, approximate=False).astype(jnp.bfloat16)
        result = jnp.dot(activated, second, preferred_element_type=jnp.float32)
        scale = weight[:, chunk * step:(chunk + 1) * step].reshape(devices * step, 1)
        result = (result * scale).astype(jnp.bfloat16)
        result = lax.psum_scatter(result, ("section", "egroup"), scatter_dimension=0, tiled=True)
        result = lax.psum_scatter(result, "fsdp", scatter_dimension=0, tiled=True)
        outs.append(result)
    return jnp.concatenate(outs, axis=0)


def solution(mesh):
    small = (mesh.shape["section"], mesh.shape["egroup"], mesh.shape["fsdp"]) == (2, 4, 4)
    placed = (
        P(EVERY, None),
        P(EVERY, None),
        P(EVERY, None),
        P("egroup", "fsdp", "section"),
        P("egroup", "section", "fsdp"),
    )
    return jax.shard_map(
        fused if small else collective,
        mesh=mesh,
        in_specs=placed,
        out_specs=P(EVERY, None),
        check_vma=False,
    )
```

```python
import jax
import jax.numpy as jnp
from jax import lax
from jax.experimental import pallas as pl
from jax.experimental.pallas import tpu as pltpu
from jax.sharding import PartitionSpec as P

EVERY = ("section", "egroup", "fsdp")
MESH = pl.DeviceIdType.MESH


def partner(index, step):
    low = index % 2
    high = (index // 2) % 2
    if step % 2:
        index = index + 1 - 2 * low
    if step // 2:
        index = index + 2 - 4 * high
    return index


def gelu(v):
    return 0.5 * v * (1.0 + lax.erf(v * 0.7071067811865476))


def layer_kernel(
    tokens, gates, w_in, w_out, out,
    x, first, second, act, sec, plane, ready, zline, gate_all, scale,
    tz_s, tz_r, tp_s, tp_r, td_s, td_r, tc_s, tc_r, g_s, g_r, w1_s, w1_r, w2_s, w2_r,
    sec_s, sec_r, pl_s, pl_r, z_s, z_r, loc,
):
    me_s, me_g, me_f = lax.axis_index("section"), lax.axis_index("egroup"), lax.axis_index("fsdp")
    rows, width = tokens.shape
    cols = width // 4
    core = (1 - me_s, me_g, me_f)
    on_plane = [(me_s, partner(me_g, b), me_f) for b in range(4)]
    on_line = [(me_s, me_g, partner(me_f, k)) for k in range(4)]
    partners = [core] + on_plane[1:] + on_line[1:]

    barrier = pltpu.get_barrier_semaphore()
    for device in partners:
        pl.semaphore_signal(barrier, inc=1, device_id=device, device_id_type=MESH)
    pl.semaphore_wait(barrier, len(partners))

    def remote(src, dst, send, recv, device):
        return pltpu.make_async_remote_copy(
            src_ref=src, dst_ref=dst, send_sem=send, recv_sem=recv, device_id=device, device_id_type=MESH
        )

    def block(a, b, k):
        return x.at[a * 4 + b, pl.ds(k * rows, rows), :]

    def piece(weight, p):
        return pl.ds(pl.multiple_of(p * (weight // 4), 128), weight // 4)

    hid = w_in.shape[2]
    inner = ((me_f + 1) // 2) % 2
    is_inner = inner == 1
    token_next = remote(tokens, block(0, 0, 1), tz_s.at[1], tz_r.at[1], on_line[1])
    own_across = remote(tokens, block(0, 0, 3), tz_s.at[3], tz_r.at[3], on_line[3])
    end_across = remote(block(0, 0, 1), block(0, 0, 2), tz_s.at[2], tz_r.at[2], on_line[3])
    near_out = remote(block(0, 0, 3), block(0, 0, 2), tz_s.at[4], tz_r.at[2], on_line[1])
    far_out = remote(block(0, 0, 2), block(0, 0, 3), tz_s.at[5], tz_r.at[3], on_line[1])

    def landed(k):
        return remote(tokens, block(0, 0, k), tz_s.at[0], tz_r.at[k], on_line[1])

    def token_plane(b, k, own=False):
        return remote(
            tokens if own else block(0, 0, k), block(0, b, k), tp_s.at[b, k], tp_r.at[b, k], on_plane[b]
        )

    def half(b, k, part):
        return x.at[b, pl.ds(k * rows + part * (rows // 2), rows // 2), :]

    def token_corner(part, k):
        return remote(
            half(1 + part, k, part), half(3, k, part), td_s.at[part, k], td_r.at[part, k], on_plane[2 - part]
        )

    def token_core(b, k, own=False):
        return remote(
            tokens if own else block(0, b, k), block(1, b, k), tc_s.at[b, k], tc_r.at[b, k], core
        )

    gate_line = [None] + [
        remote(gates, gate_all.at[0, k], g_s.at[0, k], g_r.at[0, k], on_line[k]) for k in range(1, 4)
    ]
    gate_plane = {
        (b, k): remote(
            gates if k == 0 else gate_all.at[0, k],
            gate_all.at[b, k],
            g_s.at[b, k],
            g_r.at[b, k],
            on_plane[b],
        )
        for b in range(1, 4)
        for k in range(4)
    }
    first_line = [None] + [
        remote(
            w_in.at[0, :, piece(hid, partner(me_f, k))], first.at[me_f], w1_s.at[k], w1_r.at[k], on_line[k]
        )
        for k in range(1, 4)
    ]
    second_line = [None] + [
        remote(
            w_out.at[0, piece(hid, partner(me_f, k)), :], second.at[k], w2_s.at[k], w2_r.at[k], on_line[k]
        )
        for k in range(1, 4)
    ]
    own_first = pltpu.make_async_copy(w_in.at[0, :, piece(hid, me_f)], first.at[me_f], loc.at[0])
    own_second = pltpu.make_async_copy(w_out.at[0, piece(hid, me_f), :], second.at[0], loc.at[1])

    token_next.start()

    @pl.when(is_inner)
    def _():
        own_across.start()

    for b in (1, 2):
        token_plane(b, 0, True).start()
    token_core(0, 0, True).start()
    for k in (3, 2, 1):
        gate_line[k].start()
    own_first.start()
    own_second.start()
    x[0, 0:rows, :] = tokens[...]
    for b in range(1, 4):
        gate_plane[b, 0].start()
    gate_all[0, 0] = gates[...]

    def spread(k, onward):
        landed(k).wait_recv()

        @pl.when(is_inner)
        def _():
            onward.start()

        for b in (1, 2):
            token_plane(b, k).start()
        token_core(0, k).start()

    def corner(k):
        for part in range(2):
            token_plane(1 + part, k).wait_recv()
            token_corner(part, k).start()
            token_core(1 + part, k).start()

    second_in = 2 + inner
    third_in = 5 - second_in
    spread(1, end_across)
    corner(0)
    spread(second_in, near_out)
    corner(1)
    spread(third_in, far_out)
    for k in (3, 2, 1):
        first_line[k].start()
    corner(second_in)
    corner(third_in)
    for k in (0, 1, second_in, third_in):
        for part in range(2):
            token_corner(part, k).wait_recv()
        token_core(3, k).start()
    for k in (1, 2, 3):
        first_line[k].wait_recv()
    own_first.wait()
    for k in (1, 2, 3):
        second_line[k].start()
    for k in (1, 2, 3):
        gate_line[k].wait_recv()
        for b in range(1, 4):
            gate_plane[b, k].start()

    def project(group, carry):
        hidden = jnp.dot(x[group], first[...].reshape(width, cols), preferred_element_type=jnp.float32)
        act[group] = gelu(hidden).astype(jnp.bfloat16)
        return carry

    lax.fori_loop(0, 4, project, 0)
    for k in range(4):
        for b in range(4):
            token_core(b, k).wait_recv()
    lax.fori_loop(4, 8, project, 0)
    for k in range(4):
        for b in range(4):
            token_core(b, k).wait_send()
        for part in range(2):
            token_plane(1 + part, k).wait_send()
            token_corner(part, k).wait_send()
    token_next.wait_send()

    @pl.when(is_inner)
    def _():
        for copy in (own_across, end_across, near_out, far_out):
            copy.wait_send()

    own_second.wait()

    def lane(j):
        return pl.ds(j * cols, cols)

    sec_copy = [remote(x.at[4:8, :, lane(j)], sec.at[j], sec_s.at[j], sec_r.at[j], core) for j in range(4)]
    def part_rows(part):
        return pl.ds(part * 2 * rows, 2 * rows)

    plane_copy = {}
    for j in range(4):
        for part in range(2):
            near, far = 1 + part, 2 - part
            for i, (group, device) in enumerate(((near, near), (3, near), (far, far))):
                plane_copy[j, part, i] = remote(
                    x.at[group, part_rows(part), lane(j)],
                    plane.at[j, i, part_rows(part), :],
                    pl_s.at[j, part * 3 + i],
                    pl_r.at[j, part * 3 + i],
                    on_plane[device],
                )
    line_copy = {
        (j, k): remote(
            ready.at[j, k], zline.at[j ^ k, k - 1], z_s.at[j, k], z_r.at[j ^ k, k], on_line[k]
        )
        for j in range(4)
        for k in range(1, 4)
    }

    def expand(j):
        if j:
            second_line[j].wait_recv()

        def body(group, carry):
            value = jnp.dot(act[group], second[j], preferred_element_type=jnp.float32)
            x[group, :, j * cols:(j + 1) * cols] = value.astype(jnp.bfloat16)
            return carry

        lax.fori_loop(4, 8, body, 0)
        sec_copy[j].start()
        lax.fori_loop(0, 4, body, 0)

    def join_halves(j):
        if j == 0:
            for b in range(4):
                for k in range(4):
                    if b:
                        gate_plane[b, k].wait_recv()
                    scale[b, k * rows:(k + 1) * rows, :] = jnp.transpose(gate_all[b, k])
        sec_copy[j].wait_recv()
        for b in (3, 1, 2, 0):
            total = x[b, :, j * cols:(j + 1) * cols].astype(jnp.float32) + sec[j, b].astype(jnp.float32)
            total = total * scale[b, :, b:b + 1]
            x[b, :, j * cols:(j + 1) * cols] = total.astype(jnp.bfloat16)
            if b == 3:
                plane_copy[j, 0, 1].start()
                plane_copy[j, 1, 1].start()
            elif b:
                plane_copy[j, b - 1, 0].start()

    def pass_on(j):
        for part in range(2):
            group, span = 2 - part, slice(part * 2 * rows, (part + 1) * 2 * rows)
            plane_copy[j, part, 1].wait_recv()
            total = x[group, span, j * cols:(j + 1) * cols].astype(jnp.float32)
            total = total + plane[j, 1, span, :].astype(jnp.float32)
            x[group, span, j * cols:(j + 1) * cols] = total.astype(jnp.bfloat16)
            plane_copy[j, part, 2].start()

    def join_experts(j):
        for part in range(2):
            plane_copy[j, part, 0].wait_recv()
            plane_copy[j, part, 2].wait_recv()
        for k in (3, 2, 1, 0):
            span = slice(k * rows, (k + 1) * rows)
            total = x[0, span, j * cols:(j + 1) * cols].astype(jnp.float32)
            for i in (0, 2):
                total = total + plane[j, i, span, :].astype(jnp.float32)
            ready[j, k] = total.astype(jnp.bfloat16)
            if k:
                line_copy[j, k].start()

    for step in range(7):
        if 0 <= step - 1 < 4:
            join_halves(step - 1)
        if 0 <= step - 2 < 4:
            pass_on(step - 2)
        if 0 <= step - 3 < 4:
            join_experts(step - 3)
        if step < 4:
            expand(step)
    for j in range(4):
        total = ready[j, 0].astype(jnp.float32)
        for k in range(1, 4):
            line_copy[j ^ k, k].wait_recv()
            total = total + zline[j, k - 1].astype(jnp.float32)
        out[:, pl.ds(pl.multiple_of(partner(me_f, j) * cols, 128), cols)] = total.astype(jnp.bfloat16)

    for copy in gate_line[1:] + first_line[1:] + second_line[1:] + sec_copy:
        copy.wait_send()
    for copy in list(gate_plane.values()) + list(plane_copy.values()) + list(line_copy.values()):
        copy.wait_send()


def fused(tokens, expert_ids, gate_weights, w_in, w_out):
    rows, width = tokens.shape
    steps = jnp.arange(8, dtype=jnp.int32)
    expert = jnp.where(steps < 4, steps ^ lax.axis_index("egroup"), -1)[:, None]
    gates = sum(jnp.where(expert_ids[:, i][None, :] == expert, gate_weights[:, i][None, :], 0.0) for i in range(2))
    cols, hid = width // 4, w_in.shape[2] // 4
    wide, vmem, dma = jnp.bfloat16, pltpu.VMEM, pltpu.SemaphoreType.DMA
    return pl.pallas_call(
        layer_kernel,
        out_shape=jax.ShapeDtypeStruct((rows, width), wide),
        in_specs=[
            pl.BlockSpec(memory_space=pltpu.VMEM),
            pl.BlockSpec(memory_space=pltpu.VMEM),
            pl.BlockSpec(memory_space=pl.ANY),
            pl.BlockSpec(memory_space=pl.ANY),
        ],
        out_specs=pl.BlockSpec(memory_space=pltpu.VMEM),
        scratch_shapes=[
            vmem((8, 4 * rows, width), wide),
            vmem((4, cols, hid), wide),
            vmem((4, hid, cols), wide),
            vmem((8, 4 * rows, hid), wide),
            vmem((4, 4, 4 * rows, cols), wide),
            vmem((4, 3, 4 * rows, cols), wide),
            vmem((4, 4, rows, cols), wide),
            vmem((4, 3, rows, cols), wide),
            vmem((4, 4, 8, rows), jnp.float32),
            vmem((4, 4 * rows, 8), jnp.float32),
        ]
        + [dma((6,)), dma((4,)), dma((4, 4)), dma((4, 4)), dma((2, 4)), dma((2, 4)), dma((4, 4)), dma((4, 4))]
        + [dma((4, 4)), dma((4, 4))]
        + [dma((4,)), dma((4,)), dma((4,)), dma((4,)), dma((4,)), dma((4,))]
        + [dma((4, 6)), dma((4, 6)), dma((4, 4)), dma((4, 4)), dma((2,))],
        compiler_params=pltpu.CompilerParams(
            collective_id=0, has_side_effects=True, vmem_limit_bytes=58 * 2**20
        ),
    )(tokens, gates, w_in, w_out)


def collective(tokens, expert_ids, gate_weights, w_in, w_out):
    rows, width = tokens.shape
    devices = lax.axis_size("section") * lax.axis_size("egroup") * lax.axis_size("fsdp")
    chunks = 4
    step = rows // chunks
    mine = lax.axis_index("egroup")
    first = lax.all_to_all(w_in[0], "fsdp", split_axis=1, concat_axis=0, tiled=True)
    second = lax.all_to_all(w_out[0], "fsdp", split_axis=0, concat_axis=1, tiled=True)
    ids = lax.all_gather(expert_ids, EVERY, axis=0)
    gates = lax.all_gather(gate_weights, EVERY, axis=0)
    weight = jnp.sum(jnp.where(ids == mine, gates, 0.0), axis=2)
    outs = []
    for chunk in range(chunks):
        part = tokens[chunk * step:(chunk + 1) * step]
        part = lax.all_gather(part, "fsdp", axis=0, tiled=True)
        part = lax.all_gather(part, ("section", "egroup"), axis=0, tiled=True)
        hidden = jnp.dot(part, first, preferred_element_type=jnp.float32)
        activated = jax.nn.gelu(hidden, approximate=False).astype(jnp.bfloat16)
        result = jnp.dot(activated, second, preferred_element_type=jnp.float32)
        scale = weight[:, chunk * step:(chunk + 1) * step].reshape(devices * step, 1)
        result = (result * scale).astype(jnp.bfloat16)
        result = lax.psum_scatter(result, ("section", "egroup"), scatter_dimension=0, tiled=True)
        result = lax.psum_scatter(result, "fsdp", scatter_dimension=0, tiled=True)
        outs.append(result)
    return jnp.concatenate(outs, axis=0)


def solution(mesh):
    small = (mesh.shape["section"], mesh.shape["egroup"], mesh.shape["fsdp"]) == (2, 4, 4)
    placed = (
        P(EVERY, None),
        P(EVERY, None),
        P(EVERY, None),
        P("egroup", "fsdp", "section"),
        P("egroup", "section", "fsdp"),
    )
    return jax.shard_map(
        fused if small else collective,
        mesh=mesh,
        in_specs=placed,
        out_specs=P(EVERY, None),
        check_vma=False,
    )
```
